32 devices in a mesh: seq: 4 (over z), exp: 8 (over y, x, core).
Axes of the slice: x: 2, y: 2, z: 4, core: 2. Of those that a mesh axis runs over, the one named last changes fastest.
Arguments:
- queries: bfloat16 [8, 16, 8192], P('exp', 'seq'), may hold values from -8 to 8
- key_rows: bfloat16 [8, 16, 512], P('exp', 'seq'), may hold values from -8 to 8
- values: bfloat16 [8, 16, 512], P('exp', 'seq'), may hold values from -6 to 6
- residual: bfloat16 [8, 16, 4096], P('exp'), may hold values from -4 to 4
- out_proj: bfloat16 [8192, 4096], P('seq'), may hold values from -0.25 to 0.25
- norm_gain: bfloat16 [4096], replicated, may hold values from 0.5 to 1.5
- expert_ids: int32 [8, 16, 8], P('exp'), may hold values from 0 to 15, all different within a row; in each aligned block of 16 rows (0 to 15, 16 to 31, ..., all dimensions but the last counted through in order) at most 10 rows name the same one
- route_weights: float32 [8, 16, 8], P('exp'), may hold values from 0.05 to 0.35
- gate_weight: bfloat16 [4, 8, 4096, 512], P('seq', 'exp'), may hold values from -0.09375 to 0.09375
- up_weight: bfloat16 [4, 8, 4096, 512], P('seq', 'exp'), may hold values from -0.09375 to 0.09375
- down_weight: bfloat16 [16, 1024, 4096], P('exp', None, 'seq'), may hold values from -0.1875 to 0.1875
Outputs:
- layer_out: bfloat16 [8, 16, 4096], P('exp', None, 'seq')
The draws below stay inside these ranges and needn't reach their ends.
Inputs may be any that keep to these rules, and one draw needn't show every extreme that they name: `expert_ids`: each token names 8 different experts. In each query block no expert is named by more than 10 of its tokens, and in some block an expert is named by exactly 10.
All inputs are finite; a program needn't handle non-finite values.
Results may differ from the reference program's by a relative error of at most 0.018.
Values may be sent and summed in bfloat16 or wider, within the bound.
No kernel may reach another device: no remote copies, remote signals or barrier semaphores. Data moves between devices by JAX's collectives and lax.ppermute only.
A program may use at most 64 MiB of HBM per device.

```python
import math
import jax
import jax.numpy as jnp
import numpy as np
from jax import lax

D = 4096
HEADS = 64
KV_HEADS = 4
HEAD_DIM = 128
FF = 1024
TOPK = 8
BLOCKS = 8
COLUMN = 16
TOKENS = 128
EXPERTS = 16
SLICES = 2
FF_DEV = 512
ATT = 8192
CAP = 10


def draw_queries(key, part):
    values = jnp.clip(1.5 * jax.random.normal(jax.random.fold_in(key, 11), (TOKENS, HEADS, HEAD_DIM), jnp.float32), -8.0, 8.0)
    return values.reshape(BLOCKS, COLUMN, HEADS * HEAD_DIM).astype(jnp.bfloat16)


def draw_key_rows(key, part):
    values = jnp.clip(1.5 * jax.random.normal(jax.random.fold_in(key, 12), (TOKENS, KV_HEADS, HEAD_DIM), jnp.float32), -8.0, 8.0)
    return values.reshape(BLOCKS, COLUMN, KV_HEADS * HEAD_DIM).astype(jnp.bfloat16)


def shard_levels(key, dims, pieces, low, high):
    loudness = 1.0
    for dim, shards_of in pieces:
        heights = jax.random.uniform(jax.random.fold_in(jax.random.fold_in(key, 6), dim), (shards_of,), jnp.float32, low / len(pieces), high / len(pieces))
        loudness = loudness * jnp.repeat(jnp.exp(heights), dims[dim] // shards_of).reshape((-1,) + (1,) * (len(dims) - 1 - dim))
    return loudness


def assign_block(own_key, own, number, rows, number_of, top, reach, skew):
    ranking = jax.random.permutation(own_key, number_of)
    heavy_load, ordinary = portions_of(number_of, rows * top, reach, skew, True), portions_of(number_of, rows * top, reach, skew, False)
    places = jnp.arange(number_of)

    def named(sizes, rotation):
        used = int((sizes > 0).sum())
        fixed = max(1, used // 4)
        shifted = fixed + (places - fixed + rotation * (used - fixed)) % max(1, number_of - fixed)
        return jnp.zeros((number_of,), jnp.int32).at[ranking[jnp.where(places < fixed, places, shifted)]].set(jnp.asarray(sizes, jnp.int32))

    sizes = jnp.where(number % 4 == 0, named(heavy_load, number // 4), named(ordinary, number - number // 4 - 1))
    mixed = jax.random.permutation(jax.random.fold_in(own, 3), number_of)
    source_of, taker = mixed[0:number_of // 2 * 2:2], mixed[1:number_of // 2 * 2:2]
    room = jnp.minimum(sizes[source_of] - 1, reach - sizes[taker]) // 2
    room = jnp.where((source_of == ranking[0]) | (taker == ranking[0]) | (sizes[taker] == 0), 0, jnp.maximum(room, 0))
    shifted = jax.random.randint(jax.random.fold_in(own, 4), (number_of // 2,), 0, 1 << 20) % (room + 1)
    sizes = sizes.at[source_of].add(-shifted).at[taker].add(shifted)
    items = jnp.searchsorted(jnp.cumsum(sizes), jnp.arange(rows * top), side="right").astype(jnp.int32)
    grid = items.reshape(top, rows).T
    grid = grid[jax.random.permutation(jax.random.fold_in(own, 1), rows)]
    rotation = jax.random.randint(jax.random.fold_in(own, 2), (rows, 1), 0, top)
    return jnp.take_along_axis(grid, (jnp.arange(top)[None, :] + rotation) % top, axis=1)


def portions_of(number_of, total, most, slope, full):
    portions = [(1 << 20) // math.isqrt(standing ** slope) + 1 for standing in range(1, number_of + 1)]
    largest = most if full else min(most, max(-(-total // number_of), total * portions[0] // sum(portions)))
    least = 1 if total - largest >= number_of - 1 else 0
    counts, surplus = [largest] + [least] * (number_of - 1), total - largest - least * (number_of - 1)
    while surplus > 0:
        movable = [i for i in range(1, number_of) if counts[i] < largest] or [i for i in range(1, number_of) if counts[i] < most]
        mass, budget = sum([portions[i] for i in movable]), surplus
        for i in movable:
            addition = min(most - counts[i], max(1, budget * portions[i] // mass), surplus)
            counts[i] = counts[i] + addition
            surplus = surplus - addition
    return np.array(counts)


def normal_values(key, shape, width, most, shards=(), held_as=jnp.bfloat16):
    gain = shard_levels(key, shape, shards, -0.22, 0.18) if shards else 1.0
    values = jax.random.normal(key, shape, jnp.float32) * width * gain
    return jnp.minimum(jnp.maximum(values, -most), most).astype(held_as)


def setup_inputs(seed: int = 0) -> dict:
    keys = jax.random.split(jax.random.key(seed), 12)
    queries = draw_queries(jax.random.fold_in(keys[11], 71), 0)
    key_rows = draw_key_rows(jax.random.fold_in(keys[11], 71), 0)
    values = normal_values(keys[2], (BLOCKS, COLUMN, KV_HEADS * HEAD_DIM), 1.0, 6.0, ((0, 8), (1, 4)))
    residual = normal_values(keys[3], (BLOCKS, COLUMN, D), 0.5, 4.0, ((0, 8),))
    out_proj = normal_values(keys[4], (ATT, D), (4 * HEAD_DIM) ** -0.5, 0.25, ((0, 4),))
    norm_gain = jnp.clip(1.0 + 0.1 * jax.random.normal(keys[5], (D,), jnp.float32), 0.5, 1.5).astype(jnp.bfloat16)
    expert_ids_keys = jax.random.split(jax.random.fold_in(keys[6], 1), BLOCKS * COLUMN // COLUMN)
    expert_ids_turns = jax.random.permutation(jax.random.fold_in(keys[6], 3), BLOCKS * COLUMN // COLUMN)
    expert_ids = jax.vmap(lambda own, number: assign_block(jax.random.fold_in(keys[6], 2), own, number, COLUMN, EXPERTS, TOPK, CAP, 2))(expert_ids_keys, expert_ids_turns).reshape((BLOCKS, COLUMN, TOPK))
    route_weights = jnp.clip(0.05 + 0.29999999 * jax.random.uniform(keys[7], (BLOCKS, COLUMN, TOPK), jnp.float32) ** shard_levels(keys[7], (BLOCKS, COLUMN, TOPK), ((0, 8),), -0.2, 0.2), 0.05, 0.35)
    gate_weight = normal_values(keys[8], (2 * SLICES, BLOCKS, D, FF_DEV), D ** -0.5, 0.09375, ((0, 4), (1, 8)))
    up_weight = normal_values(keys[9], (2 * SLICES, BLOCKS, D, FF_DEV), D ** -0.5, 0.09375, ((0, 4), (1, 8)))
    down_weight = normal_values(keys[10], (EXPERTS, FF, D), FF ** -0.5, 0.1875, ((0, 8), (2, 4)))
    return {"queries": queries, "key_rows": key_rows, "values": values, "residual": residual, "out_proj": out_proj, "norm_gain": norm_gain, "expert_ids": expert_ids, "route_weights": route_weights, "gate_weight": gate_weight, "up_weight": up_weight, "down_weight": down_weight}


norm_eps = 1e-06

def attend_head(q_rows, k_rows, v_rows):
    scores = jnp.dot(q_rows, k_rows.T, preferred_element_type=jnp.float32) * HEAD_DIM ** (-0.5)
    position = jnp.arange(TOKENS, dtype=jnp.int32)
    allowed = position[:, None] >= position[None, :]
    scores = jnp.where(allowed, scores, -jnp.inf)
    highest = lax.optimization_barrier(jnp.max(scores, axis=1, keepdims=True))
    weights = jnp.exp(scores - highest)
    weight_sum = lax.optimization_barrier(jnp.sum(weights, axis=1, keepdims=True))
    mixed_rows = jnp.dot(weights.astype(jnp.bfloat16), v_rows, preferred_element_type=jnp.float32) / weight_sum
    return mixed_rows.astype(jnp.bfloat16)

def reference(queries, key_rows, values, residual, out_proj, norm_gain, expert_ids, route_weights, gate_weight, up_weight, down_weight):
    head_group = HEADS // KV_HEADS
    q_all = queries.reshape(TOKENS, HEADS, HEAD_DIM).transpose(1, 0, 2)
    k_all = key_rows.reshape(TOKENS, KV_HEADS, HEAD_DIM).transpose(1, 0, 2)
    v_all = values.reshape(TOKENS, KV_HEADS, HEAD_DIM).transpose(1, 0, 2)

    def one_head(number):
        return attend_head(q_all[number], k_all[number // head_group], v_all[number // head_group])
    attended = lax.map(one_head, jnp.arange(HEADS, dtype=jnp.int32))
    attended = attended.transpose(1, 0, 2).reshape(TOKENS, HEADS * HEAD_DIM)
    hidden_one = residual.reshape(TOKENS, D).astype(jnp.float32) + jnp.dot(attended, out_proj, preferred_element_type=jnp.float32)
    mean_square = lax.optimization_barrier(jnp.mean(hidden_one * hidden_one, axis=1, keepdims=True))
    normed = (hidden_one * lax.rsqrt(mean_square + norm_eps) * norm_gain.astype(jnp.float32)).astype(jnp.bfloat16)
    normed_blocks = normed.reshape(BLOCKS, COLUMN, D).astype(jnp.float32)
    flat_ids = expert_ids.reshape(BLOCKS, COLUMN * TOPK)
    onehot = (flat_ids[:, :, None] == jnp.arange(EXPERTS, dtype=jnp.int32)[None, None, :]).astype(jnp.int32)
    slot_of = lax.optimization_barrier(jnp.sum(jnp.cumsum(onehot, axis=1) * onehot, axis=2)) - 1
    flat_weights = route_weights.reshape(BLOCKS, COLUMN * TOPK).astype(jnp.float32)
    slot_range = jnp.arange(CAP, dtype=jnp.int32)
    zero_index = jnp.zeros((), jnp.int32)

    def add_expert(running, expert):
        chosen = (flat_ids == expert)[:, None, :] & (slot_of[:, None, :] == slot_range[None, :, None])
        chosen_f = chosen.astype(jnp.float32)
        token_map = chosen_f.reshape(BLOCKS, CAP, COLUMN, TOPK).sum(axis=3)
        weight_map = (chosen_f * flat_weights[:, None, :]).reshape(BLOCKS, CAP, COLUMN, TOPK).sum(axis=3)
        expert_rows = jnp.einsum('bct,btd->bcd', token_map, normed_blocks, precision=lax.Precision.HIGHEST)
        expert_rows = expert_rows.astype(jnp.bfloat16).reshape(BLOCKS * CAP, D)
        pair_index = expert // 2
        parity = expert % 2
        gate_full = lax.dynamic_slice(gate_weight, (parity * SLICES, pair_index, zero_index, zero_index), (SLICES, 1, D, FF_DEV))[:, 0]
        gate_full = gate_full.transpose(1, 0, 2).reshape(D, FF)
        up_full = lax.dynamic_slice(up_weight, (parity * SLICES, pair_index, zero_index, zero_index), (SLICES, 1, D, FF_DEV))[:, 0]
        up_full = up_full.transpose(1, 0, 2).reshape(D, FF)
        gate_vals = jnp.dot(expert_rows, gate_full, preferred_element_type=jnp.float32)
        up_vals = jnp.dot(expert_rows, up_full, preferred_element_type=jnp.float32)
        activated = (jax.nn.silu(gate_vals) * up_vals).astype(jnp.bfloat16)
        down_full = lax.dynamic_index_in_dim(down_weight, expert, 0, keepdims=False)
        expert_out = jnp.dot(activated, down_full, preferred_element_type=jnp.float32).astype(jnp.bfloat16)
        expert_out = lax.optimization_barrier(expert_out).astype(jnp.float32).reshape(BLOCKS, CAP, D)
        running = running + jnp.einsum('bct,bcd->btd', weight_map, expert_out, precision=lax.Precision.HIGHEST)
        return (running, None)
    routed, unused = lax.scan(add_expert, jnp.zeros((BLOCKS, COLUMN, D), jnp.float32), jnp.arange(EXPERTS, dtype=jnp.int32))
    return (hidden_one.reshape(BLOCKS, COLUMN, D) + routed).astype(jnp.bfloat16)
```

```python
import jax
import jax.numpy as jnp
from jax import lax
from jax.sharding import PartitionSpec as P

D = 4096
HEADS = 64
KV_HEADS = 4
HEAD_DIM = 128
FF = 1024
TOPK = 8
EXP_DEV = 2


norm_eps = 1e-06
masked_score = -1e30

def exchange(value, axis, step):
    count = lax.axis_size(axis)
    return lax.ppermute(value, axis, [(i, i ^ step) for i in range(count)])


def in_order(pieces, index):
    bit = 1
    while bit < len(pieces):
        swap = (index & bit) != 0
        pieces = [jnp.where(swap, pieces[i ^ bit], pieces[i]) for i in range(len(pieces))]
        bit *= 2
    return pieces


def compact(
    queries,
    key_rows,
    values,
    residual,
    out_proj,
    norm_gain,
    expert_ids,
    route_weights,
    gate_weight,
    up_weight,
    down_weight,
):
    seq_count = lax.axis_size("seq")
    exp_count = lax.axis_size("exp")
    s = lax.axis_index("seq")
    e = lax.axis_index("exp")
    bf16, f32 = jnp.bfloat16, jnp.float32
    tok_dev = queries.shape[1]
    column = tok_dev * seq_count
    head_dev = HEADS // seq_count
    exp_dev = down_weight.shape[0]
    experts = exp_dev * exp_count
    steps = list(range(0, exp_count, 2)) + list(range(1, exp_count, 2))
    half = exp_count // 2
    tokens = exp_count * column

    q_local = queries.reshape(tok_dev, seq_count, head_dev * HEAD_DIM)
    k_local = key_rows.reshape(tok_dev, KV_HEADS, HEAD_DIM)
    v_local = values.reshape(tok_dev, KV_HEADS, HEAD_DIM)
    reps = seq_count // KV_HEADS
    wide = jnp.concatenate(
        [q_local, jnp.repeat(k_local, reps, axis=1), jnp.repeat(v_local, reps, axis=1)], axis=2
    )
    pieces = []
    for k in range(seq_count):
        piece = lax.dynamic_index_in_dim(wide, s ^ k, 1, keepdims=False)
        pieces.append(piece if k == 0 else exchange(piece, "seq", k))
    rows = jnp.concatenate(in_order(pieces, s), axis=0)
    q_heads = rows[:, : head_dev * HEAD_DIM].reshape(column * head_dev, HEAD_DIM)

    expert_of = lax.iota(jnp.int32, experts)
    table = jnp.sum(
        jnp.where(
            expert_ids[0][:, :, None] == expert_of[None, None, :], route_weights[0][:, :, None], 0.0
        ),
        axis=1,
    )
    high = lax.reduce_precision(table, 8, 7)
    middle = lax.reduce_precision(table - high, 8, 7)
    low = table - high - middle
    lanes = 128
    packed = jnp.concatenate([high, middle, low], axis=1).astype(bf16)
    packed = jnp.pad(packed, ((0, 0), (0, -packed.shape[1] % lanes)))
    block = jnp.concatenate([rows[:, head_dev * HEAD_DIM :], packed], axis=1)
    near = jnp.concatenate(
        [block] + [exchange(block, "exp", k) for k in range(2, exp_count, 2)], axis=0
    )
    gathered = jnp.concatenate([near, exchange(near, "exp", 1)], axis=0)
    keys = gathered[:, :HEAD_DIM]
    vals = gathered[:, HEAD_DIM : 2 * HEAD_DIM]
    terms = gathered[:, 2 * HEAD_DIM : 2 * HEAD_DIM + 3 * experts].astype(f32)
    weight_of = terms[:, :experts] + terms[:, experts : 2 * experts] + terms[:, 2 * experts :]

    position = lax.iota(jnp.int32, tokens)
    step_of = position // column
    step_of = jnp.where(step_of < half, 2 * step_of, 2 * (step_of - half) + 1)
    key_pos = (e ^ step_of) * column + position % column
    query_pos = e * column + lax.iota(jnp.int32, column * head_dev) // head_dev
    scores = jnp.dot(q_heads, keys.T, preferred_element_type=f32) * (HEAD_DIM ** (-0.5))
    allowed = key_pos[None, :] <= query_pos[:, None]
    scores = jnp.where(allowed, scores, masked_score)
    top = jnp.max(scores, axis=1, keepdims=True)
    weights = jnp.where(allowed, jnp.exp(scores - top), 0.0)
    total = jnp.sum(weights, axis=1, keepdims=True)
    attended = jnp.dot(weights.astype(bf16), vals, preferred_element_type=f32) / total
    attended = attended.astype(bf16).reshape(column, head_dev * HEAD_DIM)
    projected = jnp.dot(attended, out_proj, preferred_element_type=f32)
    step = 1
    while step < seq_count:
        projected = projected + exchange(projected.astype(bf16), "seq", step).astype(f32)
        step *= 2
    hidden_one = residual[0].astype(f32) + projected
    mean_square = jnp.mean(hidden_one * hidden_one, axis=1, keepdims=True)
    normed = (hidden_one * lax.rsqrt(mean_square + norm_eps) * norm_gain.astype(f32)).astype(bf16)
    col_width = down_weight.shape[2]
    kept = lax.dynamic_slice_in_dim(hidden_one, s * col_width, col_width, 1)

    capacity = min(column, column * TOPK // experts + 2)
    slots = exp_count * capacity
    mine = lax.dynamic_slice_in_dim(weight_of, e * exp_dev, exp_dev, 1)
    named = (mine != 0.0).astype(bf16)
    before = (
        (position[None, :] < position[:, None])
        & (position[None, :] // column == position[:, None] // column)
    ).astype(bf16)
    rank = jnp.dot(before, named, preferred_element_type=f32).astype(jnp.int32)
    slot = jnp.where(mine != 0.0, (position // column * capacity)[:, None] + rank, -1)
    slot_of = lax.iota(jnp.int32, slots)
    parity = s // (seq_count // exp_dev)
    own_slot = jnp.sum(jnp.where(lax.iota(jnp.int32, exp_dev)[None, :] == parity, slot, 0), axis=1)
    pick = (slot_of[:, None] == own_slot[None, :]).astype(bf16)
    combine = jnp.concatenate(
        [
            jnp.where(slot_of[None, :] == slot[:, p : p + 1], mine[:, p : p + 1], 0.0)
            for p in range(exp_dev)
        ],
        axis=1,
    )

    near = jnp.concatenate(
        [normed] + [exchange(normed, "exp", k) for k in range(2, exp_count, 2)], axis=0
    )
    far = exchange(near, "exp", 1)
    gate_local = gate_weight[0, 0]
    up_local = up_weight[0, 0]

    def units(part):
        gate_vals = jnp.dot(part, gate_local, preferred_element_type=f32)
        up_vals = jnp.dot(part, up_local, preferred_element_type=f32)
        return (jax.nn.silu(gate_vals) * up_vals).astype(bf16)

    activated = units(jnp.concatenate([near, far], axis=0))
    activated = jnp.dot(pick, activated, preferred_element_type=f32).astype(bf16)
    pieces = [activated] + [exchange(activated, "seq", k) for k in range(1, seq_count)]
    pieces = in_order(pieces, s)
    group = seq_count // exp_dev
    outputs = jnp.concatenate(
        [
            jnp.dot(
                jnp.concatenate(pieces[p * group : (p + 1) * group], axis=1),
                down_weight[p],
                preferred_element_type=f32,
            )
            for p in range(exp_dev)
        ],
        axis=0,
    ).astype(bf16)
    routed = jnp.dot(
        combine, outputs.astype(f32), precision=lax.Precision.HIGHEST, preferred_element_type=f32
    )
    mid = half * column
    routed = routed[:mid] + exchange(routed[mid:].astype(bf16), "exp", 1).astype(f32)
    result = kept + routed[:column]
    for i in range(1, half):
        part = routed[i * column : (i + 1) * column].astype(bf16)
        result = result + exchange(part, "exp", 2 * i).astype(f32)
    return result.astype(bf16)[None]


def shards(
    queries,
    key_rows,
    values,
    residual,
    out_proj,
    norm_gain,
    expert_ids,
    route_weights,
    gate_weight,
    up_weight,
    down_weight,
):
    seq_count = lax.axis_size("seq")
    exp_count = lax.axis_size("exp")
    if down_weight.shape[0] * exp_count <= 2 * TOPK:
        return compact(
            queries,
            key_rows,
            values,
            residual,
            out_proj,
            norm_gain,
            expert_ids,
            route_weights,
            gate_weight,
            up_weight,
            down_weight,
        )
    seq_index = lax.axis_index("seq")
    exp_index = lax.axis_index("exp")
    tok_dev = queries.shape[1]
    column = tok_dev * seq_count
    head_dev = HEADS // seq_count
    score_scale = HEAD_DIM ** (-0.5)
    q_local = queries.reshape(tok_dev, seq_count, head_dev * HEAD_DIM)
    k_local = key_rows.reshape(tok_dev, KV_HEADS, HEAD_DIM)
    v_local = values.reshape(tok_dev, KV_HEADS, HEAD_DIM)
    pair_local = jnp.repeat(
        jnp.concatenate([k_local, v_local], axis=2), seq_count // KV_HEADS, axis=1
    )
    q_column, pair_column = (
        lax.all_to_all(q_local, "seq", split_axis=1, concat_axis=0, tiled=True),
        lax.all_to_all(pair_local, "seq", split_axis=1, concat_axis=0, tiled=True),
    )
    q_heads = q_column.reshape(column, head_dev, HEAD_DIM)
    pair_column = pair_column.reshape(column, 2 * HEAD_DIM)
    query_pos = exp_index * column + lax.iota(jnp.int32, column)
    last_query = exp_index * column + (column - 1)
    starting = (
        jnp.full((head_dev, column), masked_score, jnp.float32),
        jnp.zeros((head_dev, column), jnp.float32),
        jnp.zeros((head_dev, column, HEAD_DIM), jnp.float32),
    )
    shard_pair = lax.all_gather(pair_column, "exp", axis=0, tiled=True)

    def update(current):
        top_score, weight_sum, accumulated = current
        key_part = shard_pair[:, :HEAD_DIM]
        value_part = shard_pair[:, HEAD_DIM:]
        scores = (
            jnp.einsum("qhd,kd->hqk", q_heads, key_part, preferred_element_type=jnp.float32)
            * score_scale
        )
        key_pos = lax.iota(jnp.int32, shard_pair.shape[0])
        allowed = key_pos[None, :] <= query_pos[:, None]
        scores = jnp.where(allowed[None], scores, masked_score)
        new_top = jnp.maximum(top_score, jnp.max(scores, axis=2))
        weights = jnp.where(allowed[None], jnp.exp(scores - new_top[:, :, None]), 0.0)
        weight_sum = jnp.sum(weights, axis=2)
        accumulated = jnp.einsum(
            "hqk,kd->hqd",
            weights.astype(jnp.bfloat16),
            value_part,
            preferred_element_type=jnp.float32,
        )
        return (new_top, weight_sum, accumulated)

    def unchanged(current):
        return current

    top_score, weight_sum, accumulated = lax.cond(
        jnp.int32(0) <= last_query, update, unchanged, starting
    )
    attended = (accumulated / weight_sum[:, :, None]).astype(jnp.bfloat16)
    projected = jnp.einsum(
        "hqd,hde->qe",
        attended,
        out_proj.reshape(head_dev, HEAD_DIM, D),
        preferred_element_type=jnp.float32,
    )
    col_width = down_weight.shape[2]
    summed = lax.psum(projected.astype(jnp.bfloat16), "seq").astype(jnp.float32)
    hidden_one = residual[0].astype(jnp.float32) + summed
    mean_square = jnp.mean(hidden_one * hidden_one, axis=1, keepdims=True)
    normed = (
        hidden_one * lax.rsqrt(mean_square + norm_eps) * norm_gain.astype(jnp.float32)
    ).astype(jnp.bfloat16)
    kept = lax.dynamic_slice_in_dim(hidden_one, seq_index * col_width, col_width, 1)
    experts = EXP_DEV * exp_count
    capacity = min(column, column * TOPK // experts + 2)
    route_ids = expert_ids[0]
    flat_ids = route_ids.reshape(-1)
    onehot = (flat_ids[:, None] == lax.iota(jnp.int32, experts)[None, :]).astype(jnp.int32)
    slot_of = (jnp.sum(jnp.cumsum(onehot, axis=0) * onehot, axis=1) - 1).reshape(column, TOPK)
    slices = seq_count // 2
    parity = seq_index // slices
    target = route_ids // 2 * capacity + slot_of
    chosen = route_ids % 2 == parity
    places = lax.iota(jnp.int32, exp_count * capacity)
    dispatch_map = jnp.any(
        (target[:, :, None] == places[None, None, :]) & chosen[:, :, None], axis=1
    ).astype(jnp.bfloat16)
    gate_local = gate_weight[0, 0]
    up_local = up_weight[0, 0]
    rows_full = jnp.einsum("tp,td->pd", dispatch_map, normed, preferred_element_type=jnp.float32)
    rows_full = rows_full.astype(jnp.bfloat16).reshape(exp_count, capacity, D)
    rows_in = lax.all_to_all(rows_full, "exp", split_axis=0, concat_axis=0, tiled=True)
    gate_vals = jnp.einsum("ecd,df->ecf", rows_in, gate_local, preferred_element_type=jnp.float32)
    up_vals = jnp.einsum("ecd,df->ecf", rows_in, up_local, preferred_element_type=jnp.float32)
    activated = (jax.nn.silu(gate_vals) * up_vals).astype(jnp.bfloat16)
    whole = lax.all_gather(activated, "seq", axis=2, tiled=True)
    first = jnp.einsum(
        "ecf,fo->eco", whole[:, :, :FF], down_weight[0], preferred_element_type=jnp.float32
    )
    second = jnp.einsum(
        "ecf,fo->eco", whole[:, :, FF:], down_weight[1], preferred_element_type=jnp.float32
    )
    outputs = jnp.stack([first, second], axis=2).astype(jnp.bfloat16)
    returned = lax.all_to_all(outputs, "exp", split_axis=0, concat_axis=0, tiled=True)
    index_map = route_ids // 2 * (capacity * 2) + slot_of * 2 + route_ids % 2
    positions = lax.iota(jnp.int32, exp_count * capacity * 2)
    combine_table = jnp.sum(
        jnp.where(
            index_map[:, :, None] == positions[None, None, :], route_weights[0][:, :, None], 0.0
        ),
        axis=1,
    )
    routed = jnp.dot(
        combine_table,
        returned.astype(jnp.float32).reshape(exp_count * capacity * 2, col_width),
        precision=lax.Precision.HIGHEST,
        preferred_element_type=jnp.float32,
    )
    return (kept + routed).astype(jnp.bfloat16)[None]


def solution(mesh):
    in_specs = (
        P("exp", "seq", None),
        P("exp", "seq", None),
        P("exp", "seq", None),
        P("exp", None, None),
        P("seq", None),
        P(),
        P("exp", None, None),
        P("exp", None, None),
        P("seq", "exp", None, None),
        P("seq", "exp", None, None),
        P("exp", None, "seq"),
    )
    out_specs = P("exp", None, "seq")
    return jax.shard_map(shards, mesh=mesh, in_specs=in_specs, out_specs=out_specs, check_vma=False)
```

```python
import jax
import jax.numpy as jnp
from jax import lax
from jax.experimental import pallas as pl
from jax.experimental.pallas import tpu as pltpu
from jax.sharding import PartitionSpec as P

D = 4096
HEADS = 64
KV_HEADS = 4
HEAD_DIM = 128
FF = 1024
TOPK = 8
EXP_DEV = 2


norm_eps = 1e-06
masked_score = -1e30


def fetch(sources, after, cuts=1):
    shapes = [(source.shape[0] // cuts,) + source.shape[1:] for source in sources for _ in range(cuts)]

    def body(*refs):
        n = len(sources)
        copies = []
        for i, shape in enumerate(shapes):
            source = refs[i // cuts].at[pl.ds(i % cuts * shape[0], shape[0])]
            target, sem = refs[n + 1 + i], refs[n + 1 + n * cuts].at[i]
            copies.append(pltpu.make_async_copy(source, target, sem))
        for copy in copies:
            copy.start()
        for copy in copies:
            copy.wait()

    moved = sum(source.size * source.dtype.itemsize for source in sources)
    return pl.pallas_call(
        body,
        out_shape=[pltpu.VMEM(shape, sources[0].dtype) for shape in shapes],
        in_specs=[pl.BlockSpec(memory_space=pltpu.HBM)] * len(sources)
        + [pl.BlockSpec(memory_space=pl.ANY)],
        out_specs=[pl.BlockSpec(memory_space=pltpu.VMEM)] * len(shapes),
        scratch_shapes=[pltpu.SemaphoreType.DMA((len(shapes),))],
        compiler_params=pltpu.CompilerParams(vmem_limit_bytes=1 << 20),
        cost_estimate=pl.CostEstimate(flops=0, transcendentals=0, bytes_accessed=2 * moved),
    )(*[in_hbm(source) for source in sources], after)


def in_hbm(array):
    return pltpu.with_memory_space_constraint(array, pltpu.HBM)


def in_vmem(array):
    return pltpu.with_memory_space_constraint(array, pltpu.VMEM)


def local_call(body, outs, *operands, flops=0, scratch=(), streamed=(), limit=8 << 20):
    moved = sum(a.size * a.dtype.itemsize for a in operands + tuple(streamed))
    spec = pl.BlockSpec(memory_space=pltpu.VMEM)
    return pl.pallas_call(
        body,
        out_shape=[pltpu.VMEM(shape, dtype) for shape, dtype in outs],
        in_specs=[spec] * len(operands)
        + [pl.BlockSpec(memory_space=pltpu.HBM)] * len(streamed),
        out_specs=[spec] * len(outs),
        scratch_shapes=list(scratch),
        compiler_params=pltpu.CompilerParams(vmem_limit_bytes=limit),
        cost_estimate=pl.CostEstimate(flops=flops, transcendentals=0, bytes_accessed=moved),
    )(*[in_vmem(a) for a in operands], *[in_hbm(a) for a in streamed])


def column_tile(width):
    return next(tile for tile in (512, 256, 128, width) if width % tile == 0)


def attend_body(rows_ref, pairs_ref, *refs):
    weight_hbm, wide_ref, sent_ref, held_ref, weight_ref, sems = refs
    width = wide_ref.shape[1]
    tile = column_tile(width)
    copies = []
    for i in range(width // tile):
        cols = pl.ds(i * tile, tile)
        copies.append(
            pltpu.make_async_copy(weight_hbm.at[:, cols], weight_ref.at[:, cols], sems.at[i])
        )
        copies[i].start()
    column = rows_ref.shape[0]
    heads = rows_ref.shape[1] // HEAD_DIM
    seq_count, exp_count, e = lax.axis_size("seq"), lax.axis_size("exp"), lax.axis_index("exp")
    tok_dev = column // seq_count
    q = jnp.concatenate(
        [rows_ref[:, h * HEAD_DIM : (h + 1) * HEAD_DIM] for h in range(heads)], axis=0
    )
    keys = pairs_ref[:, :HEAD_DIM]
    vals = pairs_ref[:, HEAD_DIM : 2 * HEAD_DIM]
    scores = lax.dot_general(
        q, keys, (((1,), (1,)), ((), ())), preferred_element_type=jnp.float32
    ) * (HEAD_DIM ** (-0.5))
    row = lax.broadcasted_iota(jnp.int32, scores.shape, 1)
    key_pos = gathered_pos(row, tok_dev, exp_count, column)
    query_pos = e * column + lax.broadcasted_iota(jnp.int32, scores.shape, 0) % column
    allowed = key_pos <= query_pos
    scores = jnp.where(allowed, scores, masked_score)
    top = jnp.max(scores, axis=1, keepdims=True)
    weights_of = jnp.where(allowed, jnp.exp(scores - top), 0.0)
    total = jnp.sum(weights_of, axis=1, keepdims=True)
    mixed = jnp.dot(weights_of.astype(jnp.bfloat16), vals, preferred_element_type=jnp.float32)
    mixed = (mixed / total).astype(jnp.bfloat16)
    for h in range(heads):
        held_ref[:, h * HEAD_DIM : (h + 1) * HEAD_DIM] = mixed[h * column : (h + 1) * column]
    for i, copy in enumerate(copies):
        copy.wait()
        cols = pl.ds(i * tile, tile)
        out = jnp.dot(held_ref[...], weight_ref[:, cols], preferred_element_type=jnp.float32)
        wide_ref[:, cols] = out
        sent_ref[:, cols] = out.astype(sent_ref.dtype)


def gathered_pos(row, tok_dev, exp_count, column):
    group = row // tok_dev
    return group % exp_count * column + group // exp_count * tok_dev + row % tok_dev


def units_body(rows_ref, gate_ref, up_ref, out_ref):
    width = gate_ref.shape[1]
    tile = min(256, column_tile(width))

    def step(i, carry):
        cols = pl.ds(pl.multiple_of(i * tile, tile), tile)
        gate = jnp.dot(rows_ref[...], gate_ref[:, cols], preferred_element_type=jnp.float32)
        up = jnp.dot(rows_ref[...], up_ref[:, cols], preferred_element_type=jnp.float32)
        out_ref[:, cols] = (gate / (1.0 + jnp.exp(-gate)) * up).astype(out_ref.dtype)
        return carry

    lax.fori_loop(0, width // tile, step, 0)


def down_body(rows_ref, weight_ref, out_ref):
    count, _, width = weight_ref.shape
    tile = min(256, column_tile(width))

    def step(i, carry):
        cols = pl.ds(pl.multiple_of(i * tile, tile), tile)
        for p in range(count):
            out = jnp.dot(rows_ref[p], weight_ref[p, :, cols], preferred_element_type=jnp.float32)
            out_ref[p, :, cols] = out.astype(out_ref.dtype)
        return carry

    lax.fori_loop(0, width // tile, step, 0)


def exchange(value, axis, step):
    count = lax.axis_size(axis)
    return lax.ppermute(value, axis, [(i, i ^ step) for i in range(count)])


def in_order(pieces, index):
    bit = 1
    while bit < len(pieces):
        swap = (index & bit) != 0
        pieces = [jnp.where(swap, pieces[i ^ bit], pieces[i]) for i in range(len(pieces))]
        bit *= 2
    return pieces


def compact(
    queries,
    key_rows,
    values,
    residual,
    out_proj,
    norm_gain,
    expert_ids,
    route_weights,
    gate_weight,
    up_weight,
    down_weight,
):
    seq_count = lax.axis_size("seq")
    exp_count = lax.axis_size("exp")
    s = lax.axis_index("seq")
    e = lax.axis_index("exp")
    bf16, f32 = jnp.bfloat16, jnp.float32
    tok_dev = queries.shape[1]
    column = tok_dev * seq_count
    head_dev = HEADS // seq_count
    exp_dev = down_weight.shape[0]
    experts = exp_dev * exp_count
    half = exp_count // 2
    tokens = exp_count * column

    width = head_dev * HEAD_DIM
    q_rows = queries[0]
    pieces = []
    for k in range(seq_count):
        piece = lax.dynamic_slice_in_dim(q_rows, (s ^ k) * width, width, 1)
        pieces.append(piece if k == 0 else exchange(piece, "seq", k))

    expert_of = lax.iota(jnp.int32, experts)
    own_ids = lax.dynamic_slice_in_dim(expert_ids[0], s * tok_dev, tok_dev, 0)
    own_weights = lax.dynamic_slice_in_dim(route_weights[0], s * tok_dev, tok_dev, 0)
    table = jnp.sum(
        jnp.where(own_ids[:, :, None] == expert_of[None, None, :], own_weights[:, :, None], 0.0),
        axis=1,
    )
    high = lax.reduce_precision(table, 8, 7)
    middle = lax.reduce_precision(table - high, 8, 7)
    low = table - high - middle
    packed = jnp.concatenate([high, middle, low], axis=1).astype(bf16)
    packed = jnp.pad(packed, ((0, 0), (0, -packed.shape[1] % 128)))

    reps = seq_count // KV_HEADS
    parts = []
    for j in range(seq_count):
        cut = slice(j // reps * HEAD_DIM, (j // reps + 1) * HEAD_DIM)
        parts.append(jnp.concatenate([key_rows[0][:, cut], values[0][:, cut], packed], axis=1))
    parts = jnp.stack(parts, axis=0)
    parts = jnp.broadcast_to(parts[:, None], (seq_count, exp_count) + parts.shape[1:])
    parts = parts.reshape((seq_count * exp_count,) + parts.shape[2:])
    gathered = lax.all_to_all(parts, ("seq", "exp"), split_axis=0, concat_axis=0, tiled=True)
    gathered = gathered.reshape(tokens, gathered.shape[2])
    rows = jnp.concatenate(in_order(pieces, s), axis=0)
    row = lax.iota(jnp.int32, tokens)
    key_pos = gathered_pos(row, tok_dev, exp_count, column)
    position = row
    step_of = position // column
    step_of = jnp.where(step_of < half, 2 * step_of, 2 * (step_of - half) + 1)
    place = (e ^ step_of) * column + position % column
    reorder = (place[:, None] == key_pos[None, :]).astype(bf16)
    terms = jnp.dot(reorder, gathered[:, 2 * HEAD_DIM :], preferred_element_type=f32)
    weight_of = (
        terms[:, :experts] + terms[:, experts : 2 * experts] + terms[:, 2 * experts : 3 * experts]
    )

    projected, sent = local_call(
        attend_body,
        [((column, D), f32), ((column, D), bf16)],
        rows,
        gathered[:, : 2 * HEAD_DIM],
        flops=2 * column * out_proj.size,
        scratch=[
            pltpu.VMEM((column, width), bf16),
            pltpu.VMEM(out_proj.shape, bf16),
            pltpu.SemaphoreType.DMA((D // column_tile(D),)),
        ],
        streamed=[out_proj],
        limit=24 << 20,
    )
    step = 1
    while step < seq_count:
        projected = projected + exchange(sent, "seq", step).astype(f32)
        sent = projected.astype(bf16)
        step *= 2
    hidden_one = residual[0].astype(f32) + projected
    mean_square = jnp.mean(hidden_one * hidden_one, axis=1, keepdims=True)
    normed = (hidden_one * lax.rsqrt(mean_square + norm_eps) * norm_gain.astype(f32)).astype(bf16)
    col_width = down_weight.shape[2]
    kept = lax.dynamic_slice_in_dim(hidden_one, s * col_width, col_width, 1)

    capacity = min(column, column * TOPK // experts + 2)
    slots = exp_count * capacity
    mine = lax.dynamic_slice_in_dim(weight_of, e * exp_dev, exp_dev, 1)
    named = (mine != 0.0).astype(bf16)
    before = (
        (position[None, :] < position[:, None])
        & (position[None, :] // column == position[:, None] // column)
    ).astype(bf16)
    rank = jnp.dot(before, named, preferred_element_type=f32).astype(jnp.int32)
    slot = jnp.where(mine != 0.0, (position // column * capacity)[:, None] + rank, -1)
    slot_of = lax.iota(jnp.int32, slots)
    parity = s // (seq_count // exp_dev)
    own_slot = jnp.sum(jnp.where(lax.iota(jnp.int32, exp_dev)[None, :] == parity, slot, 0), axis=1)
    pick = (slot_of[:, None] == own_slot[None, :]).astype(bf16)
    combine = jnp.concatenate(
        [
            jnp.where(slot_of[None, :] == slot[:, p : p + 1], mine[:, p : p + 1], 0.0)
            for p in range(exp_dev)
        ],
        axis=1,
    )

    near = [normed] + [exchange(normed, "exp", k) for k in range(2, exp_count, 2)]
    gate_local, up_local = fetch([gate_weight[0, 0], up_weight[0, 0]], normed)
    near = jnp.concatenate(near, axis=0)
    far = exchange(near, "exp", 1)

    def units(part):
        return local_call(
            units_body,
            [((part.shape[0], gate_local.shape[1]), bf16)],
            part,
            gate_local,
            up_local,
            flops=4 * part.shape[0] * gate_local.size,
        )[0]

    activated = jnp.concatenate([units(near), units(far)], axis=0)
    activated = jnp.dot(pick, activated, preferred_element_type=f32).astype(bf16)
    pieces = [activated] + [exchange(activated, "seq", k) for k in range(1, seq_count)]
    (down_local,) = fetch([down_weight], activated)
    pieces = in_order(pieces, s)
    group = seq_count // exp_dev
    rows_in = jnp.stack(
        [jnp.concatenate(pieces[p * group : (p + 1) * group], axis=1) for p in range(exp_dev)], axis=0
    )
    (outputs,) = local_call(
        down_body,
        [((exp_dev, slots, col_width), bf16)],
        rows_in,
        down_local,
        flops=2 * slots * down_weight.size,
    )
    outputs = outputs.reshape(exp_dev * slots, col_width)
    routed = jnp.dot(
        combine, outputs.astype(f32), precision=lax.Precision.HIGHEST, preferred_element_type=f32
    )
    mid = half * column
    routed = routed[:mid] + exchange(routed[mid:].astype(bf16), "exp", 1).astype(f32)
    result = kept + routed[:column]
    for i in range(1, half):
        part = routed[i * column : (i + 1) * column].astype(bf16)
        result = result + exchange(part, "exp", 2 * i).astype(f32)
    return result.astype(bf16)[None]


def shards(
    queries,
    key_rows,
    values,
    residual,
    out_proj,
    norm_gain,
    expert_ids,
    route_weights,
    gate_weight,
    up_weight,
    down_weight,
):
    seq_count = lax.axis_size("seq")
    exp_count = lax.axis_size("exp")
    if down_weight.shape[0] * exp_count <= 2 * TOPK:
        return compact(
            queries,
            key_rows,
            values,
            residual,
            out_proj,
            norm_gain,
            expert_ids,
            route_weights,
            gate_weight,
            up_weight,
            down_weight,
        )
    seq_index = lax.axis_index("seq")
    exp_index = lax.axis_index("exp")
    tok_dev = queries.shape[1]
    column = tok_dev * seq_count
    head_dev = HEADS // seq_count
    score_scale = HEAD_DIM ** (-0.5)
    q_local = queries.reshape(tok_dev, seq_count, head_dev * HEAD_DIM)
    k_local = key_rows.reshape(tok_dev, KV_HEADS, HEAD_DIM)
    v_local = values.reshape(tok_dev, KV_HEADS, HEAD_DIM)
    pair_local = jnp.repeat(
        jnp.concatenate([k_local, v_local], axis=2), seq_count // KV_HEADS, axis=1
    )
    q_column, pair_column = (
        lax.all_to_all(q_local, "seq", split_axis=1, concat_axis=0, tiled=True),
        lax.all_to_all(pair_local, "seq", split_axis=1, concat_axis=0, tiled=True),
    )
    q_heads = q_column.reshape(column, head_dev, HEAD_DIM)
    pair_column = pair_column.reshape(column, 2 * HEAD_DIM)
    query_pos = exp_index * column + lax.iota(jnp.int32, column)
    last_query = exp_index * column + (column - 1)
    starting = (
        jnp.full((head_dev, column), masked_score, jnp.float32),
        jnp.zeros((head_dev, column), jnp.float32),
        jnp.zeros((head_dev, column, HEAD_DIM), jnp.float32),
    )
    shard_pair = lax.all_gather(pair_column, "exp", axis=0, tiled=True)

    def update(current):
        top_score, weight_sum, accumulated = current
        key_part = shard_pair[:, :HEAD_DIM]
        value_part = shard_pair[:, HEAD_DIM:]
        scores = (
            jnp.einsum("qhd,kd->hqk", q_heads, key_part, preferred_element_type=jnp.float32)
            * score_scale
        )
        key_pos = lax.iota(jnp.int32, shard_pair.shape[0])
        allowed = key_pos[None, :] <= query_pos[:, None]
        scores = jnp.where(allowed[None], scores, masked_score)
        new_top = jnp.maximum(top_score, jnp.max(scores, axis=2))
        weights = jnp.where(allowed[None], jnp.exp(scores - new_top[:, :, None]), 0.0)
        weight_sum = jnp.sum(weights, axis=2)
        accumulated = jnp.einsum(
            "hqk,kd->hqd",
            weights.astype(jnp.bfloat16),
            value_part,
            preferred_element_type=jnp.float32,
        )
        return (new_top, weight_sum, accumulated)

    def unchanged(current):
        return current

    _, weight_sum, accumulated = lax.cond(jnp.int32(0) <= last_query, update, unchanged, starting)
    attended = (accumulated / weight_sum[:, :, None]).astype(jnp.bfloat16)
    projected = jnp.einsum(
        "hqd,hde->qe",
        attended,
        out_proj.reshape(head_dev, HEAD_DIM, D),
        preferred_element_type=jnp.float32,
    )
    col_width = down_weight.shape[2]
    summed = lax.psum(projected.astype(jnp.bfloat16), "seq").astype(jnp.float32)
    hidden_one = residual[0].astype(jnp.float32) + summed
    mean_square = jnp.mean(hidden_one * hidden_one, axis=1, keepdims=True)
    normed = (
        hidden_one * lax.rsqrt(mean_square + norm_eps) * norm_gain.astype(jnp.float32)
    ).astype(jnp.bfloat16)
    kept = lax.dynamic_slice_in_dim(hidden_one, seq_index * col_width, col_width, 1)
    experts = EXP_DEV * exp_count
    capacity = min(column, column * TOPK // experts + 2)
    route_ids = expert_ids[0]
    flat_ids = route_ids.reshape(-1)
    onehot = (flat_ids[:, None] == lax.iota(jnp.int32, experts)[None, :]).astype(jnp.int32)
    slot_of = (jnp.sum(jnp.cumsum(onehot, axis=0) * onehot, axis=1) - 1).reshape(column, TOPK)
    slices = seq_count // 2
    parity = seq_index // slices
    target = route_ids // 2 * capacity + slot_of
    chosen = route_ids % 2 == parity
    places = lax.iota(jnp.int32, exp_count * capacity)
    dispatch_map = jnp.any(
        (target[:, :, None] == places[None, None, :]) & chosen[:, :, None], axis=1
    ).astype(jnp.bfloat16)
    gate_local = gate_weight[0, 0]
    up_local = up_weight[0, 0]
    rows_full = jnp.einsum("tp,td->pd", dispatch_map, normed, preferred_element_type=jnp.float32)
    rows_full = rows_full.astype(jnp.bfloat16).reshape(exp_count, capacity, D)
    rows_in = lax.all_to_all(rows_full, "exp", split_axis=0, concat_axis=0, tiled=True)
    gate_vals = jnp.einsum("ecd,df->ecf", rows_in, gate_local, preferred_element_type=jnp.float32)
    up_vals = jnp.einsum("ecd,df->ecf", rows_in, up_local, preferred_element_type=jnp.float32)
    activated = (jax.nn.silu(gate_vals) * up_vals).astype(jnp.bfloat16)
    whole = lax.all_gather(activated, "seq", axis=2, tiled=True)
    first = jnp.einsum(
        "ecf,fo->eco", whole[:, :, :FF], down_weight[0], preferred_element_type=jnp.float32
    )
    second = jnp.einsum(
        "ecf,fo->eco", whole[:, :, FF:], down_weight[1], preferred_element_type=jnp.float32
    )
    outputs = jnp.stack([first, second], axis=2).astype(jnp.bfloat16)
    returned = lax.all_to_all(outputs, "exp", split_axis=0, concat_axis=0, tiled=True)
    index_map = route_ids // 2 * (capacity * 2) + slot_of * 2 + route_ids % 2
    positions = lax.iota(jnp.int32, exp_count * capacity * 2)
    combine_table = jnp.sum(
        jnp.where(
            index_map[:, :, None] == positions[None, None, :], route_weights[0][:, :, None], 0.0
        ),
        axis=1,
    )
    routed = jnp.dot(
        combine_table,
        returned.astype(jnp.float32).reshape(exp_count * capacity * 2, col_width),
        precision=lax.Precision.HIGHEST,
        preferred_element_type=jnp.float32,
    )
    return (kept + routed).astype(jnp.bfloat16)[None]


def solution(mesh):
    in_specs = (
        P("exp", "seq", None),
        P("exp", "seq", None),
        P("exp", "seq", None),
        P("exp", None, None),
        P("seq", None),
        P(),
        P("exp", None, None),
        P("exp", None, None),
        P("seq", "exp", None, None),
        P("seq", "exp", None, None),
        P("exp", None, "seq"),
    )
    out_specs = P("exp", None, "seq")
    return jax.shard_map(
        shards, mesh=mesh, in_specs=in_specs, out_specs=out_specs, check_vma=False
    )
```

```python
import functools

import jax
import jax.numpy as jnp
from jax import lax
from jax.experimental import pallas as pl
from jax.experimental.pallas import tpu as pltpu
from jax.sharding import PartitionSpec as P

D = 4096
HEADS = 64
KV_HEADS = 4
HEAD_DIM = 128
FF = 1024
TOPK = 8
EXP_DEV = 2


norm_eps = 1e-06
masked_score = -1e30


def fetch(sources, after, cuts=1):
    shapes = [(source.shape[0] // cuts,) + source.shape[1:] for source in sources for _ in range(cuts)]

    def body(*refs):
        n = len(sources)
        copies = []
        for i, shape in enumerate(shapes):
            source = refs[i // cuts].at[pl.ds(i % cuts * shape[0], shape[0])]
            target, sem = refs[n + 1 + i], refs[n + 1 + n * cuts].at[i]
            copies.append(pltpu.make_async_copy(source, target, sem))
        for copy in copies:
            copy.start()
        for copy in copies:
            copy.wait()

    moved = sum(source.size * source.dtype.itemsize for source in sources)
    return pl.pallas_call(
        body,
        out_shape=[pltpu.VMEM(shape, sources[0].dtype) for shape in shapes],
        in_specs=[pl.BlockSpec(memory_space=pltpu.HBM)] * len(sources)
        + [pl.BlockSpec(memory_space=pl.ANY)],
        out_specs=[pl.BlockSpec(memory_space=pltpu.VMEM)] * len(shapes),
        scratch_shapes=[pltpu.SemaphoreType.DMA((len(shapes),))],
        compiler_params=pltpu.CompilerParams(vmem_limit_bytes=1 << 20),
        cost_estimate=pl.CostEstimate(flops=0, transcendentals=0, bytes_accessed=2 * moved),
    )(*[in_hbm(source) for source in sources], after)


def in_hbm(array):
    return pltpu.with_memory_space_constraint(array, pltpu.HBM)


def in_vmem(array):
    return pltpu.with_memory_space_constraint(array, pltpu.VMEM)


def local_call(body, outs, *operands, flops=0, scratch=(), streamed=(), limit=8 << 20):
    moved = sum(a.size * a.dtype.itemsize for a in operands + tuple(streamed))
    spec = pl.BlockSpec(memory_space=pltpu.VMEM)
    return pl.pallas_call(
        body,
        out_shape=[pltpu.VMEM(shape, dtype) for shape, dtype in outs],
        in_specs=[spec] * len(operands)
        + [pl.BlockSpec(memory_space=pltpu.HBM)] * len(streamed),
        out_specs=[spec] * len(outs),
        scratch_shapes=list(scratch),
        compiler_params=pltpu.CompilerParams(vmem_limit_bytes=limit),
        cost_estimate=pl.CostEstimate(flops=flops, transcendentals=0, bytes_accessed=moved),
    )(*[in_vmem(a) for a in operands], *[in_hbm(a) for a in streamed])


def column_tile(width):
    return next(tile for tile in (512, 256, 128, width) if width % tile == 0)


def prepare_body(experts, q_hbm, k_hbm, v_hbm, ids_hbm, weights_hbm, *refs):
    *q_outs, parts_ref, k_ref, v_ref, ids_ref, weights_ref, sems = refs
    seq_count, s = lax.axis_size("seq"), lax.axis_index("seq")
    exp_count = lax.axis_size("exp")
    tok_dev, width = q_outs[0].shape
    copies = [
        pltpu.make_async_copy(source, target, sems.at[i])
        for i, (source, target) in enumerate(
            [(ids_hbm, ids_ref), (weights_hbm, weights_ref), (k_hbm, k_ref), (v_hbm, v_ref)]
        )
    ]
    for k, q_out in enumerate(q_outs):
        cut = pl.ds(pl.multiple_of((s ^ k) * width, 128), width)
        copies.append(pltpu.make_async_copy(q_hbm.at[:, cut], q_out, sems.at[4 + k]))
    for copy in copies:
        copy.start()
    copies[0].wait()
    copies[1].wait()

    lanes = parts_ref.shape[2] - 2 * HEAD_DIM
    count = ids_ref.shape[1]
    line = lax.broadcasted_iota(jnp.int32, (lanes, count), 0)
    table = jnp.zeros(line.shape, jnp.float32)
    for j in range(ids_ref.shape[0]):
        named = ids_ref[j : j + 1, :] == line % experts
        table = table + jnp.where(named, weights_ref[j : j + 1, :], 0.0)
    high = table.astype(jnp.bfloat16).astype(jnp.float32)
    middle = (table - high).astype(jnp.bfloat16).astype(jnp.float32)
    low = table - high - middle
    term = line // experts
    packed = jnp.where(
        term == 0, high, jnp.where(term == 1, middle, jnp.where(term == 2, low, 0.0))
    ).astype(jnp.bfloat16)
    turn = lax.broadcasted_iota(jnp.int32, (count, count), 0) + s * tok_dev
    turn = (turn == lax.broadcasted_iota(jnp.int32, (count, count), 1)).astype(jnp.bfloat16)
    own = lax.dot_general(
        turn, packed, (((1,), (1,)), ((), ())), preferred_element_type=jnp.float32
    )
    own = own[:tok_dev].astype(jnp.bfloat16)
    copies[2].wait()
    copies[3].wait()
    reps = seq_count // KV_HEADS
    for j in range(seq_count):
        cut = slice(j // reps * HEAD_DIM, (j // reps + 1) * HEAD_DIM)
        part = jnp.concatenate([k_ref[:, cut], v_ref[:, cut], own], axis=1)
        for i in range(exp_count):
            parts_ref[j * exp_count + i] = part
    for copy in copies[4:]:
        copy.wait()


def attend_body(rows_ref, pairs_ref, *refs):
    weight_hbm, wide_ref, sent_ref, held_ref, weight_ref, sems = refs
    width = wide_ref.shape[1]
    tile = column_tile(width)
    copies = []
    for i in range(width // tile):
        cols = pl.ds(i * tile, tile)
        copies.append(
            pltpu.make_async_copy(weight_hbm.at[:, cols], weight_ref.at[:, cols], sems.at[i])
        )
        copies[i].start()
    column = rows_ref.shape[0]
    heads = rows_ref.shape[1] // HEAD_DIM
    seq_count, exp_count, e = lax.axis_size("seq"), lax.axis_size("exp"), lax.axis_index("exp")
    tok_dev = column // seq_count
    q = jnp.concatenate(
        [rows_ref[:, h * HEAD_DIM : (h + 1) * HEAD_DIM] for h in range(heads)], axis=0
    )
    keys = pairs_ref[:, :HEAD_DIM]
    vals = pairs_ref[:, HEAD_DIM : 2 * HEAD_DIM]
    scores = lax.dot_general(
        q, keys, (((1,), (1,)), ((), ())), preferred_element_type=jnp.float32
    ) * (HEAD_DIM ** (-0.5))
    row = lax.broadcasted_iota(jnp.int32, scores.shape, 1)
    key_pos = gathered_pos(row, tok_dev, exp_count, column)
    query_pos = e * column + lax.broadcasted_iota(jnp.int32, scores.shape, 0) % column
    allowed = key_pos <= query_pos
    scores = jnp.where(allowed, scores, masked_score)
    top = jnp.max(scores, axis=1, keepdims=True)
    weights_of = jnp.where(allowed, jnp.exp(scores - top), 0.0)
    total = jnp.sum(weights_of, axis=1, keepdims=True)
    mixed = jnp.dot(weights_of.astype(jnp.bfloat16), vals, preferred_element_type=jnp.float32)
    mixed = (mixed / total).astype(jnp.bfloat16)
    for h in range(heads):
        held_ref[:, h * HEAD_DIM : (h + 1) * HEAD_DIM] = mixed[h * column : (h + 1) * column]
    for i, copy in enumerate(copies):
        copy.wait()
        cols = pl.ds(i * tile, tile)
        out = jnp.dot(held_ref[...], weight_ref[:, cols], preferred_element_type=jnp.float32)
        wide_ref[:, cols] = out
        sent_ref[:, cols] = out.astype(sent_ref.dtype)


def gathered_pos(row, tok_dev, exp_count, column):
    group = row // tok_dev
    return group % exp_count * column + group // exp_count * tok_dev + row % tok_dev


def units_body(rows_ref, gate_ref, up_ref, out_ref):
    width = gate_ref.shape[1]
    tile = min(256, column_tile(width))

    def step(i, carry):
        cols = pl.ds(pl.multiple_of(i * tile, tile), tile)
        gate = jnp.dot(rows_ref[...], gate_ref[:, cols], preferred_element_type=jnp.float32)
        up = jnp.dot(rows_ref[...], up_ref[:, cols], preferred_element_type=jnp.float32)
        out_ref[:, cols] = (gate / (1.0 + jnp.exp(-gate)) * up).astype(out_ref.dtype)
        return carry

    lax.fori_loop(0, width // tile, step, 0)


def down_body(rows_ref, weight_ref, combine_ref, near_ref, far_ref):
    count, _, width = weight_ref.shape
    tile = min(256, column_tile(width))
    half = near_ref.shape[0]
    high = combine_ref[...].astype(jnp.bfloat16)
    rest = combine_ref[...] - high.astype(jnp.float32)
    middle = rest.astype(jnp.bfloat16)
    low = (rest - middle.astype(jnp.float32)).astype(jnp.bfloat16)

    def step(i, carry):
        cols = pl.ds(pl.multiple_of(i * tile, tile), tile)
        outs = [
            jnp.dot(rows_ref[p], weight_ref[p, :, cols], preferred_element_type=jnp.float32)
            for p in range(count)
        ]
        outs = jnp.concatenate(outs, axis=0).astype(jnp.bfloat16)
        total = sum(
            jnp.dot(term, outs, preferred_element_type=jnp.float32) for term in (low, middle, high)
        )
        near_ref[:, cols] = total[:half]
        far_ref[:, cols] = total[half:].astype(far_ref.dtype)
        return carry

    lax.fori_loop(0, width // tile, step, 0)


def exchange(value, axis, step):
    count = lax.axis_size(axis)
    return lax.ppermute(value, axis, [(i, i ^ step) for i in range(count)])


def in_order(pieces, index):
    bit = 1
    while bit < len(pieces):
        swap = (index & bit) != 0
        pieces = [jnp.where(swap, pieces[i ^ bit], pieces[i]) for i in range(len(pieces))]
        bit *= 2
    return pieces


def compact(
    queries,
    key_rows,
    values,
    residual,
    out_proj,
    norm_gain,
    expert_ids,
    route_weights,
    gate_weight,
    up_weight,
    down_weight,
):
    seq_count = lax.axis_size("seq")
    exp_count = lax.axis_size("exp")
    s = lax.axis_index("seq")
    e = lax.axis_index("exp")
    bf16, f32 = jnp.bfloat16, jnp.float32
    tok_dev = queries.shape[1]
    column = tok_dev * seq_count
    head_dev = HEADS // seq_count
    exp_dev = down_weight.shape[0]
    experts = exp_dev * exp_count
    half = exp_count // 2
    tokens = exp_count * column

    width = head_dev * HEAD_DIM
    lanes = 3 * experts + -3 * experts % 128
    pair = 2 * HEAD_DIM + lanes
    sources = [
        queries[0],
        key_rows[0],
        values[0],
        expert_ids[0].T,
        route_weights[0].T,
    ]
    *pieces, parts = pl.pallas_call(
        functools.partial(prepare_body, experts),
        out_shape=[pltpu.VMEM((tok_dev, width), bf16)] * seq_count
        + [pltpu.VMEM((seq_count * exp_count, tok_dev, pair), bf16)],
        in_specs=[pl.BlockSpec(memory_space=pltpu.HBM)] * len(sources),
        out_specs=[pl.BlockSpec(memory_space=pltpu.VMEM)] * (seq_count + 1),
        scratch_shapes=[pltpu.VMEM(a.shape, a.dtype) for a in sources[1:]]
        + [pltpu.SemaphoreType.DMA((4 + seq_count,))],
        compiler_params=pltpu.CompilerParams(vmem_limit_bytes=2 << 20),
    )(*[in_hbm(a) for a in sources])
    gathered = lax.all_to_all(parts, ("seq", "exp"), split_axis=0, concat_axis=0, tiled=True)
    gathered = gathered.reshape(tokens, gathered.shape[2])
    pieces = pieces[:1] + [exchange(pieces[k], "seq", k) for k in range(1, seq_count)]
    rows = jnp.concatenate(in_order(pieces, s), axis=0)

    row = lax.iota(jnp.int32, tokens)
    key_pos = gathered_pos(row, tok_dev, exp_count, column)
    position = row
    step_of = position // column
    step_of = jnp.where(step_of < half, 2 * step_of, 2 * (step_of - half) + 1)
    place = (e ^ step_of) * column + position % column
    reorder = (place[:, None] == key_pos[None, :]).astype(bf16)
    terms = jnp.dot(reorder, gathered[:, 2 * HEAD_DIM :], preferred_element_type=f32)
    weight_of = (
        terms[:, :experts] + terms[:, experts : 2 * experts] + terms[:, 2 * experts : 3 * experts]
    )

    projected, sent = local_call(
        attend_body,
        [((column, D), f32), ((column, D), bf16)],
        rows,
        gathered[:, : 2 * HEAD_DIM],
        flops=2 * column * out_proj.size,
        scratch=[
            pltpu.VMEM((column, width), bf16),
            pltpu.VMEM(out_proj.shape, bf16),
            pltpu.SemaphoreType.DMA((D // column_tile(D),)),
        ],
        streamed=[out_proj],
        limit=24 << 20,
    )
    gate_local, gain = fetch([gate_weight[0, 0], norm_gain], sent)
    step = 1
    while step < seq_count:
        arrived = exchange(sent, "seq", step)
        projected = projected + arrived.astype(f32)
        sent = projected.astype(bf16)
        if step == 1:
            (up_local,) = fetch([up_weight[0, 0]], sent)
        step *= 2
    hidden_one = residual[0].astype(f32) + projected
    mean_square = jnp.mean(hidden_one * hidden_one, axis=1, keepdims=True)
    normed = (hidden_one * lax.rsqrt(mean_square + norm_eps) * gain.astype(f32)).astype(bf16)
    col_width = down_weight.shape[2]
    kept = lax.dynamic_slice_in_dim(hidden_one, s * col_width, col_width, 1)

    capacity = min(column, column * TOPK // experts + 2)
    slots = exp_count * capacity
    mine = lax.dynamic_slice_in_dim(weight_of, e * exp_dev, exp_dev, 1)
    named = (mine != 0.0).astype(bf16)
    before = (
        (position[None, :] < position[:, None])
        & (position[None, :] // column == position[:, None] // column)
    ).astype(bf16)
    rank = jnp.dot(before, named, preferred_element_type=f32).astype(jnp.int32)
    slot = jnp.where(mine != 0.0, (position // column * capacity)[:, None] + rank, -1)
    slot_of = lax.iota(jnp.int32, slots)
    parity = s // (seq_count // exp_dev)
    own_slot = jnp.sum(jnp.where(lax.iota(jnp.int32, exp_dev)[None, :] == parity, slot, 0), axis=1)
    pick = (slot_of[:, None] == own_slot[None, :]).astype(bf16)
    combine = jnp.concatenate(
        [
            jnp.where(slot_of[None, :] == slot[:, p : p + 1], mine[:, p : p + 1], 0.0)
            for p in range(exp_dev)
        ],
        axis=1,
    )

    near = [normed] + [exchange(normed, "exp", k) for k in range(2, exp_count, 2)]
    near = jnp.concatenate(near, axis=0)
    far = exchange(near, "exp", 1)

    def units(part):
        return local_call(
            units_body,
            [((part.shape[0], gate_local.shape[1]), bf16)],
            part,
            gate_local,
            up_local,
            flops=4 * part.shape[0] * gate_local.size,
        )[0]

    activated = jnp.concatenate([units(near), units(far)], axis=0)
    activated = jnp.dot(pick, activated, preferred_element_type=f32).astype(bf16)
    pieces = [activated] + [exchange(activated, "seq", k) for k in range(1, seq_count)]
    (down_local,) = fetch([down_weight], activated)
    pieces = in_order(pieces, s)
    group = seq_count // exp_dev
    rows_in = jnp.stack(
        [jnp.concatenate(pieces[p * group : (p + 1) * group], axis=1) for p in range(exp_dev)], axis=0
    )
    mid = half * column
    routed, far = local_call(
        down_body,
        [((mid, col_width), f32), ((mid, col_width), bf16)],
        rows_in,
        down_local,
        combine,
        flops=2 * slots * down_weight.size,
    )
    routed = routed + exchange(far, "exp", 1).astype(f32)
    result = kept + routed[:column]
    for i in range(1, half):
        part = routed[i * column : (i + 1) * column].astype(bf16)
        result = result + exchange(part, "exp", 2 * i).astype(f32)
    return result.astype(bf16)[None]


def shards(
    queries,
    key_rows,
    values,
    residual,
    out_proj,
    norm_gain,
    expert_ids,
    route_weights,
    gate_weight,
    up_weight,
    down_weight,
):
    seq_count = lax.axis_size("seq")
    exp_count = lax.axis_size("exp")
    if down_weight.shape[0] * exp_count <= 2 * TOPK:
        return compact(
            queries,
            key_rows,
            values,
            residual,
            out_proj,
            norm_gain,
            expert_ids,
            route_weights,
            gate_weight,
            up_weight,
            down_weight,
        )
    seq_index = lax.axis_index("seq")
    exp_index = lax.axis_index("exp")
    tok_dev = queries.shape[1]
    column = tok_dev * seq_count
    head_dev = HEADS // seq_count
    score_scale = HEAD_DIM ** (-0.5)
    q_local = queries.reshape(tok_dev, seq_count, head_dev * HEAD_DIM)
    k_local = key_rows.reshape(tok_dev, KV_HEADS, HEAD_DIM)
    v_local = values.reshape(tok_dev, KV_HEADS, HEAD_DIM)
    pair_local = jnp.repeat(
        jnp.concatenate([k_local, v_local], axis=2), seq_count // KV_HEADS, axis=1
    )
    q_column, pair_column = (
        lax.all_to_all(q_local, "seq", split_axis=1, concat_axis=0, tiled=True),
        lax.all_to_all(pair_local, "seq", split_axis=1, concat_axis=0, tiled=True),
    )
    q_heads = q_column.reshape(column, head_dev, HEAD_DIM)
    pair_column = pair_column.reshape(column, 2 * HEAD_DIM)
    query_pos = exp_index * column + lax.iota(jnp.int32, column)
    last_query = exp_index * column + (column - 1)
    starting = (
        jnp.full((head_dev, column), masked_score, jnp.float32),
        jnp.zeros((head_dev, column), jnp.float32),
        jnp.zeros((head_dev, column, HEAD_DIM), jnp.float32),
    )
    shard_pair = lax.all_gather(pair_column, "exp", axis=0, tiled=True)

    def update(current):
        top_score, weight_sum, accumulated = current
        key_part = shard_pair[:, :HEAD_DIM]
        value_part = shard_pair[:, HEAD_DIM:]
        scores = (
            jnp.einsum("qhd,kd->hqk", q_heads, key_part, preferred_element_type=jnp.float32)
            * score_scale
        )
        key_pos = lax.iota(jnp.int32, shard_pair.shape[0])
        allowed = key_pos[None, :] <= query_pos[:, None]
        scores = jnp.where(allowed[None], scores, masked_score)
        new_top = jnp.maximum(top_score, jnp.max(scores, axis=2))
        weights = jnp.where(allowed[None], jnp.exp(scores - new_top[:, :, None]), 0.0)
        weight_sum = jnp.sum(weights, axis=2)
        accumulated = jnp.einsum(
            "hqk,kd->hqd",
            weights.astype(jnp.bfloat16),
            value_part,
            preferred_element_type=jnp.float32,
        )
        return (new_top, weight_sum, accumulated)

    def unchanged(current):
        return current

    _, weight_sum, accumulated = lax.cond(jnp.int32(0) <= last_query, update, unchanged, starting)
    attended = (accumulated / weight_sum[:, :, None]).astype(jnp.bfloat16)
    projected = jnp.einsum(
        "hqd,hde->qe",
        attended,
        out_proj.reshape(head_dev, HEAD_DIM, D),
        preferred_element_type=jnp.float32,
    )
    col_width = down_weight.shape[2]
    summed = lax.psum(projected.astype(jnp.bfloat16), "seq").astype(jnp.float32)
    hidden_one = residual[0].astype(jnp.float32) + summed
    mean_square = jnp.mean(hidden_one * hidden_one, axis=1, keepdims=True)
    normed = (
        hidden_one * lax.rsqrt(mean_square + norm_eps) * norm_gain.astype(jnp.float32)
    ).astype(jnp.bfloat16)
    kept = lax.dynamic_slice_in_dim(hidden_one, seq_index * col_width, col_width, 1)
    experts = EXP_DEV * exp_count
    capacity = min(column, column * TOPK // experts + 2)
    route_ids = expert_ids[0]
    flat_ids = route_ids.reshape(-1)
    onehot = (flat_ids[:, None] == lax.iota(jnp.int32, experts)[None, :]).astype(jnp.int32)
    slot_of = (jnp.sum(jnp.cumsum(onehot, axis=0) * onehot, axis=1) - 1).reshape(column, TOPK)
    slices = seq_count // 2
    parity = seq_index // slices
    target = route_ids // 2 * capacity + slot_of
    chosen = route_ids % 2 == parity
    places = lax.iota(jnp.int32, exp_count * capacity)
    dispatch_map = jnp.any(
        (target[:, :, None] == places[None, None, :]) & chosen[:, :, None], axis=1
    ).astype(jnp.bfloat16)
    gate_local = gate_weight[0, 0]
    up_local = up_weight[0, 0]
    rows_full = jnp.einsum("tp,td->pd", dispatch_map, normed, preferred_element_type=jnp.float32)
    rows_full = rows_full.astype(jnp.bfloat16).reshape(exp_count, capacity, D)
    rows_in = lax.all_to_all(rows_full, "exp", split_axis=0, concat_axis=0, tiled=True)
    gate_vals = jnp.einsum("ecd,df->ecf", rows_in, gate_local, preferred_element_type=jnp.float32)
    up_vals = jnp.einsum("ecd,df->ecf", rows_in, up_local, preferred_element_type=jnp.float32)
    activated = (jax.nn.silu(gate_vals) * up_vals).astype(jnp.bfloat16)
    whole = lax.all_gather(activated, "seq", axis=2, tiled=True)
    first = jnp.einsum(
        "ecf,fo->eco", whole[:, :, :FF], down_weight[0], preferred_element_type=jnp.float32
    )
    second = jnp.einsum(
        "ecf,fo->eco", whole[:, :, FF:], down_weight[1], preferred_element_type=jnp.float32
    )
    outputs = jnp.stack([first, second], axis=2).astype(jnp.bfloat16)
    returned = lax.all_to_all(outputs, "exp", split_axis=0, concat_axis=0, tiled=True)
    index_map = route_ids // 2 * (capacity * 2) + slot_of * 2 + route_ids % 2
    positions = lax.iota(jnp.int32, exp_count * capacity * 2)
    combine_table = jnp.sum(
        jnp.where(
            index_map[:, :, None] == positions[None, None, :], route_weights[0][:, :, None], 0.0
        ),
        axis=1,
    )
    routed = jnp.dot(
        combine_table,
        returned.astype(jnp.float32).reshape(exp_count * capacity * 2, col_width),
        precision=lax.Precision.HIGHEST,
        preferred_element_type=jnp.float32,
    )
    return (kept + routed).astype(jnp.bfloat16)[None]


def solution(mesh):
    in_specs = (
        P("exp", "seq", None),
        P("exp", "seq", None),
        P("exp", "seq", None),
        P("exp", None, None),
        P("seq", None),
        P(),
        P("exp", None, None),
        P("exp", None, None),
        P("seq", "exp", None, None),
        P("seq", "exp", None, None),
        P("exp", None, "seq"),
    )
    out_specs = P("exp", None, "seq")
    return jax.shard_map(
        shards, mesh=mesh, in_specs=in_specs, out_specs=out_specs, check_vma=False
    )
```
